32 devices in a mesh: grp: 4 (over y, x), seq: 8 (over z, core).
Axes of the slice: x: 2, y: 2, z: 4, core: 2. Of those that a mesh axis runs over, the one named last changes fastest.
Arguments:
- query_proj: bfloat16 [4096, 2048], P(('grp', 'seq')), may hold values from -6 to 6
- key_proj: bfloat16 [4096, 2048], P(('grp', 'seq')), may hold values from -13 to 13
- value_proj: bfloat16 [4096, 2048], P(('grp', 'seq')), may hold values from -6 to 6
- log_decay: float32 [4096, 16], P(('grp', 'seq')), may hold values from -1 to 0, as said below
- write_rate: float32 [4096, 16], P(('grp', 'seq')), may hold values from 0 to 1, as said below
- gate_proj: bfloat16 [4096, 2048], P(('grp', 'seq')), may hold values from -6 to 6
- norm_gain: float32 [128], replicated, may hold values from 0.1 to 1.9
- initial_state: float32 [16, 128, 128], replicated, may hold values from -0.125 to 0.125
Outputs:
- mixed: bfloat16 [4096, 2048], P(('grp', 'seq'))
The draws below stay inside these ranges and needn't reach their ends.
Inputs may be any that keep to these rules, and one draw needn't show every extreme that they name: log_decay is the logarithm of a factor in (0, 1]. write_rate is a strength in (0, 1).
All inputs are finite; a program needn't handle non-finite values.
Results may differ from the reference program's by a relative error of at most 0.0011.
Values sent between devices are 32-bit elements; how exact they have to be, the bound alone decides.
No kernel may reach another device: no remote copies, remote signals or barrier semaphores. Data moves between devices by JAX's collectives and lax.ppermute only.
A program may use at most 320 MiB of HBM per device.

```python
import math
import jax
import jax.numpy as jnp
from jax import lax

ATTENTION_UNITS = 16
DK = 128
DV = 128
BLOCK = 64
TOK_DEV = 128
EPOCH_SAMPLES = 4096


def decay_pair(key):
    address_vectors = jax.random.split(jax.random.fold_in(key, 11), 11)
    head_order = jax.random.permutation(address_vectors[0], ATTENTION_UNITS)
    slow_count = ATTENTION_UNITS // 2
    middle_count = ATTENTION_UNITS // 4
    lingering_units = head_order < slow_count
    middle_units = (head_order >= slow_count) & (head_order < slow_count + middle_count)
    roughness = jnp.exp(jax.random.uniform(address_vectors[1], (EPOCH_SAMPLES, ATTENTION_UNITS), jnp.float32, -0.7, 0.7))
    device_scale = jnp.exp(jax.random.uniform(address_vectors[2], (EPOCH_SAMPLES // TOK_DEV, 1, ATTENTION_UNITS), jnp.float32, -0.7, 0.7))
    device_factor = jnp.broadcast_to(device_scale, (EPOCH_SAMPLES // TOK_DEV, TOK_DEV, ATTENTION_UNITS)).reshape(EPOCH_SAMPLES, ATTENTION_UNITS)
    fast_rate = jnp.exp(jax.random.uniform(address_vectors[3], (ATTENTION_UNITS,), jnp.float32, math.log(0.02), math.log(0.05)))
    slow_rate = jnp.exp(jax.random.uniform(address_vectors[4], (ATTENTION_UNITS,), jnp.float32, math.log(0.1), math.log(0.5))) / EPOCH_SAMPLES
    middle_rate = jnp.exp(jax.random.uniform(address_vectors[10], (ATTENTION_UNITS,), jnp.float32, math.log(0.5), math.log(1.0))) / TOK_DEV
    base_rate = jnp.where(lingering_units, slow_rate, jnp.where(middle_units, middle_rate, fast_rate))
    forgetting_exponents = -base_rate[None, :] * roughness * device_factor
    spike_indices = jax.random.randint(address_vectors[5], (3,), 0, EPOCH_SAMPLES)
    spike_indicator = jnp.any(jnp.arange(EPOCH_SAMPLES)[:, None] == spike_indices[None, :], axis=1)
    spike_forgetting = jnp.log(jax.random.uniform(address_vectors[6], (EPOCH_SAMPLES, ATTENTION_UNITS), jnp.float32, 0.65, 0.8))
    forgetting_exponents = forgetting_exponents + jnp.where(spike_indicator[:, None] & lingering_units[None, :], spike_forgetting, 0.0)
    slow_write = jnp.exp(jax.random.uniform(address_vectors[7], (ATTENTION_UNITS,), jnp.float32, math.log(0.5), math.log(1.5))) * DK / EPOCH_SAMPLES
    write_noise = jnp.exp(jax.random.uniform(address_vectors[8], (EPOCH_SAMPLES, ATTENTION_UNITS), jnp.float32, -0.5, 0.5))
    write_slow = jnp.minimum(slow_write[None, :] * write_noise, 0.9)
    write_fast = jax.random.uniform(address_vectors[9], (EPOCH_SAMPLES, ATTENTION_UNITS), jnp.float32, 0.2, 0.9)
    write_rates = jnp.where(lingering_units[None, :], write_slow, write_fast)
    return (forgetting_exponents, write_rates)


def draw_log_decay(key, part):
    return decay_pair(key)[0]


def draw_write_rate(key, part):
    return decay_pair(key)[1]


def draw_key_proj(key, part):
    address_vectors = jax.random.split(jax.random.fold_in(key, 23), 3)
    shared_direction = jax.random.truncated_normal(address_vectors[0], -3.0, 3.0, (ATTENTION_UNITS, DK), jnp.float32)
    strength = jax.random.uniform(address_vectors[1], (ATTENTION_UNITS, 1), jnp.float32, 1.2, 3.0)
    noise = jax.random.truncated_normal(address_vectors[2], -4.0, 4.0, (EPOCH_SAMPLES, ATTENTION_UNITS, DK), jnp.float32)
    keys_all = noise + (strength * shared_direction)[None, :, :]
    return keys_all.reshape(EPOCH_SAMPLES, ATTENTION_UNITS * DK).astype(jnp.bfloat16)


def steps_of(rng, dims, shards, smallest, top_value):
    def one(dim, parts):
        draws = jax.random.uniform(jax.random.fold_in(jax.random.fold_in(rng, 6), dim), (parts,), jnp.float32, smallest / len(shards), top_value / len(shards))
        return jnp.repeat(jnp.exp(draws), dims[dim] // parts).reshape((-1,) + (1,) * (len(dims) - dim - 1))

    loudness = one(*shards[0])
    for cut in shards[1:]:
        loudness = loudness * one(*cut)
    return loudness


def bell_draw(stream_key, extent, scale, limit, cuts=(), kind=jnp.bfloat16):
    factor_of = steps_of(stream_key, extent, cuts, -0.22, 0.18) if cuts else 1.0
    drawn = jax.random.normal(stream_key, extent, jnp.float32) * scale * factor_of
    return jnp.minimum(jnp.maximum(drawn, -limit), limit).astype(kind)


def setup_inputs(seed: int = 0) -> dict:
    seeds = jax.random.split(jax.random.key(seed), 9)
    return {
        "query_proj": bell_draw(seeds[0], (EPOCH_SAMPLES, ATTENTION_UNITS * DK), 1.0, 6.0, ((0, 32),)),
        "key_proj": draw_key_proj(jax.random.fold_in(seeds[8], 71), 0),
        "value_proj": bell_draw(seeds[2], (EPOCH_SAMPLES, ATTENTION_UNITS * DV), 1.0, 6.0, ((0, 32),)),
        "log_decay": draw_log_decay(jax.random.fold_in(seeds[8], 71), 0),
        "write_rate": draw_write_rate(jax.random.fold_in(seeds[8], 71), 0),
        "gate_proj": bell_draw(seeds[5], (EPOCH_SAMPLES, ATTENTION_UNITS * DV), 1.0, 6.0, ((0, 32),)),
        "norm_gain": jnp.clip(1.0 + 0.18 * jax.random.normal(seeds[6], (DV,), jnp.float32), 0.1, 1.9),
        "initial_state": bell_draw(seeds[7], (ATTENTION_UNITS, DK, DV), (ATTENTION_UNITS * DK) ** -0.5, 0.125, (), jnp.float32),
    }


HIGHEST = lax.Precision.HIGHEST

def unit_rows(entries):
    return entries * lax.rsqrt(lax.optimization_barrier(jnp.sum(entries * entries, axis=-1, keepdims=True)) + 1e-06)

def matmul(left, right):
    return jnp.einsum('...ij,...jk->...ik', left, right, precision=HIGHEST)

def inner_rows(left, right):
    return jnp.einsum('...ik,...jk->...ij', left, right, precision=HIGHEST)

def left_contract(left, right):
    return jnp.einsum('...ci,...cj->...ij', left, right, precision=HIGHEST)

def block_terms(queries, key_rows, values, decays, write_rates):
    cumulative = jnp.cumsum(decays, axis=-1)
    block_size = decays.shape[-1]
    later = lax.broadcasted_iota(jnp.int32, (block_size, block_size), 0)
    earlier = lax.broadcasted_iota(jnp.int32, (block_size, block_size), 1)
    within = later >= earlier
    before = later > earlier
    spread = cumulative[..., :, None] - cumulative[..., None, :]
    damping = jnp.where(within, jnp.exp(jnp.where(within, spread, 0.0)), 0.0)
    key_products = inner_rows(key_rows, key_rows)
    strict_part = jnp.where(before, write_rates[..., :, None] * key_products * damping, 0.0)
    unit_lower = jnp.eye(block_size, dtype=jnp.float32) + strict_part
    scaled_keys = (write_rates * jnp.exp(cumulative))[..., None] * key_rows
    scaled_values = write_rates[..., None] * values
    stacked = jnp.concatenate([scaled_keys, scaled_values], axis=-1)
    solved = lax.linalg.triangular_solve(unit_lower, stacked, left_side=True, lower=True, unit_diagonal=True)
    key_width = key_rows.shape[-1]
    erase = solved[..., :key_width]
    insert = solved[..., key_width:]
    final_log = cumulative[..., -1:]
    carried_keys = jnp.exp(final_log - cumulative)[..., None] * key_rows
    readout_mix = inner_rows(queries, key_rows) * damping
    query_scaled = jnp.exp(cumulative)[..., None] * queries
    retention = jnp.exp(final_log)[..., None]
    return (erase, insert, carried_keys, readout_mix, query_scaled, retention)

def block_apply(terms, state):
    erase, insert, carried_keys, readout_mix, query_scaled, retention = terms
    fresh_rows = insert - matmul(erase, state)
    readout = matmul(query_scaled, state) + matmul(readout_mix, fresh_rows)
    next_state = retention * state + left_contract(carried_keys, fresh_rows)
    return (readout, next_state)

def gated_norm(readout, gate, gain):
    scaled = readout * lax.rsqrt(lax.optimization_barrier(jnp.mean(readout * readout, axis=-1, keepdims=True)) + 1e-05) * gain
    return (scaled * jax.nn.silu(gate.astype(jnp.float32))).astype(jnp.bfloat16)

def reference(query_proj, key_proj, value_proj, log_decay, write_rate, gate_proj, norm_gain, initial_state):
    length = query_proj.shape[0]
    blocks = length // BLOCK

    def per_head(array, width):
        return array.reshape(blocks, BLOCK, ATTENTION_UNITS, width)
    sequence = (per_head(query_proj, DK), per_head(key_proj, DK), per_head(value_proj, DV), log_decay.reshape(blocks, BLOCK, ATTENTION_UNITS), write_rate.reshape(blocks, BLOCK, ATTENTION_UNITS), per_head(gate_proj, DV))

    def advance(state, pieces):
        query_block, key_block, value_block, decay_block, rate_block, gate_block = pieces
        queries = unit_rows(query_block.astype(jnp.float32).transpose(1, 0, 2))
        key_rows = unit_rows(key_block.astype(jnp.float32).transpose(1, 0, 2))
        values = value_block.astype(jnp.float32).transpose(1, 0, 2)
        terms = block_terms(queries, key_rows, values, decay_block.T, rate_block.T)
        readout, next_state = block_apply(terms, state)
        gated = gated_norm(readout.transpose(1, 0, 2), gate_block, norm_gain)
        return (next_state, gated.reshape(BLOCK, ATTENTION_UNITS * DV))
    final_state, mixed = lax.scan(advance, initial_state, sequence)
    return mixed.reshape(length, ATTENTION_UNITS * DV)
```

```python
import functools

import jax
import jax.numpy as jnp
from jax import lax
from jax.experimental import pallas as pl
from jax.experimental.pallas import tpu as pltpu
from jax.sharding import PartitionSpec as P

ATTENTION_UNITS = 16
DK = 128
DV = 128
HALF = ATTENTION_UNITS // 2
F32 = jnp.float32
BF16 = jnp.bfloat16
HIGHEST = lax.Precision.HIGHEST
VMEM_LIMIT = 60 * 1024 * 1024


def dot(left, right):
    return jnp.dot(left, right, preferred_element_type=F32)


def dot_t(left, right):
    return lax.dot_general(left, right, (((1,), (1,)), ((), ())), preferred_element_type=F32)


def t_dot(left, right):
    return lax.dot_general(left, right, (((0,), (0,)), ((), ())), preferred_element_type=F32)


def split(x):
    high = x.astype(BF16)
    low = (x - high.astype(F32)).astype(BF16)
    return high, low


def wide(x):
    return jnp.concatenate(split(x), axis=1)


def halves_sum(x):
    width = x.shape[1] // 2
    return x[:, :width] + x[:, width:]


def mul(left, right):
    pair = wide(left)
    high, low = split(right)
    if right.shape[1] == DK:
        row = jnp.concatenate([high, low], axis=1)
        return halves_sum(dot(pair, jnp.concatenate([row, row], axis=0)))
    return dot(pair, jnp.concatenate([high, high], axis=0)) + dot(
        pair, jnp.concatenate([low, low], axis=0)
    )


def mul_exact(left, right):
    return dot(wide(left), jnp.concatenate([right, right], axis=0))


def positions(size):
    later = lax.broadcasted_iota(jnp.int32, (size, size), 0)
    earlier = lax.broadcasted_iota(jnp.int32, (size, size), 1)
    return later, earlier


def three(x):
    first = x.astype(BF16)
    rest = x - first.astype(F32)
    second = rest.astype(BF16)
    third = (rest - second.astype(F32)).astype(BF16)
    return first, second, third


def running_sum(decays):
    later, earlier = positions(decays.shape[0])
    ones = jnp.where(later >= earlier, 1.0, 0.0).astype(BF16)
    first, second, third = three(decays)
    return dot(ones, first) + (dot(ones, second) + dot(ones, third))


def pick_half(x, side, axis):
    low = lax.slice_in_dim(x, 0, HALF, axis=axis)
    high = lax.slice_in_dim(x, HALF, 2 * HALF, axis=axis)
    return jnp.where(side == 0, low, high)


def map_kernel(side_ref, key_ref, value_ref, decay_ref, rate_ref, maps_ref, solved_ref):
    side = side_ref[0]
    length = key_ref.shape[0]
    later, earlier = positions(length)
    eye = later == earlier
    identity = jnp.where(eye, 1.0, 0.0)
    total = running_sum(decay_ref[...])
    rates = rate_ref[...]
    total_col = pick_half(total, side, 1)
    rate_col = pick_half(rates, side, 1)
    total_row = pick_half(total.T, side, 0)
    rate_row = pick_half(rates.T, side, 0)
    heads = range(HALF)
    keys = [key_ref[:, h * DK : (h + 1) * DK] for h in heads]
    values = [value_ref[:, h * DV : (h + 1) * DV] for h in heads]
    grams = [dot_t(keys[h], keys[h]) for h in heads]
    lower, unit_row, unit_col = [], [], []
    for h in heads:
        diagonal = jnp.where(eye, grams[h], 0.0)
        row = lax.rsqrt(jnp.sum(diagonal, axis=0, keepdims=True) + 1e-06)
        col = lax.rsqrt(jnp.sum(diagonal, axis=1, keepdims=True) + 1e-06)
        spread = total_col[:, h : h + 1] - total_row[h : h + 1, :]
        strict = later > earlier
        damping = jnp.exp(jnp.where(strict, spread, 0.0))
        scale = (rate_col[:, h : h + 1] * col) * row
        lower.append(jnp.where(strict, grams[h] * scale * damping, 0.0))
        unit_row.append(row)
        unit_col.append(col)
    size = 1
    inverse = [
        identity - jnp.where((later // 2) == (earlier // 2), lower[h], 0.0) for h in heads
    ]
    size = 2
    while size < length:
        band = ((later // (2 * size)) == (earlier // (2 * size))) & (
            (later // size) != (earlier // size)
        )
        inner = [mul(jnp.where(band, lower[h], 0.0), inverse[h]) for h in heads]
        outer = [mul(inverse[h], inner[h]) for h in heads]
        inverse = [inverse[h] - outer[h] for h in heads]
        size *= 2
    for h in heads:
        row = total_row[h : h + 1, :]
        rate = rate_row[h : h + 1, :]
        erase = mul_exact(inverse[h] * (rate * jnp.exp(row) * unit_row[h]), keys[h])
        insert = mul_exact(inverse[h] * rate, values[h])
        solved = jnp.concatenate([erase, insert], axis=1)
        solved_ref[h] = solved
        final = total_col[length - 1 : length, h : h + 1]
        carried = jnp.exp(final - total_col[:, h : h + 1]) * unit_col[h]
        high, low = split(solved * carried)
        moved = t_dot(keys[h], high) + t_dot(keys[h], low)
        maps_ref[h, :, :DK] = jnp.exp(final) * identity - moved[:, :DK]
        maps_ref[h, :, DK:] = moved[:, DK:]


def whole(shape):
    return pl.BlockSpec(shape, lambda i, *refs: (0,) * len(shape))


def params():
    return pltpu.CompilerParams(vmem_limit_bytes=VMEM_LIMIT)


def make_maps(side, keys, values, decays, rates):
    length = keys.shape[0]
    block = pl.BlockSpec((length, HALF * DK), lambda i, side: (0, side[0]))
    out = jax.ShapeDtypeStruct((HALF, DK, DK + DV), F32)
    solved = jax.ShapeDtypeStruct((HALF, length, DK + DV), F32)
    return pl.pallas_call(
        map_kernel,
        out_shape=(out, solved),
        grid_spec=pltpu.PrefetchScalarGridSpec(
            num_scalar_prefetch=1,
            grid=(1,),
            in_specs=[block, block, whole(decays.shape), whole(rates.shape)],
            out_specs=(whole(out.shape), whole(solved.shape)),
        ),
        compiler_params=params(),
        name="block_maps",
    )(side, keys, values, decays, rates)


def readout_kernel(side_ref, query_ref, key_ref, decay_ref, solved_ref, from_state_ref, own_ref):
    side = side_ref[0]
    length = key_ref.shape[0]
    later, earlier = positions(length)
    total = running_sum(decay_ref[...])
    total_col = pick_half(total, side, 1)
    total_row = pick_half(total.T, side, 0)
    within = later >= earlier
    for h in range(HALF):
        query = query_ref[:, h * DK : (h + 1) * DK]
        key = key_ref[:, h * DK : (h + 1) * DK]
        wide_query = query.astype(F32)
        wide_key = key.astype(F32)
        query_unit = lax.rsqrt(jnp.sum(wide_query * wide_query, axis=1, keepdims=True) + 1e-06)
        key_unit = lax.rsqrt(jnp.sum(wide_key * wide_key, axis=1, keepdims=True) + 1e-06)
        key_row = jnp.broadcast_to(key_unit, (length, DK)).T[:1, :]
        spread = total_col[:, h : h + 1] - total_row[h : h + 1, :]
        damping = jnp.exp(jnp.where(within, spread, 0.0))
        mix = jnp.where(within, dot_t(query, key) * damping * query_unit * key_row, 0.0)
        product = mul(mix, solved_ref[h])
        grown = jnp.exp(total_col[:, h : h + 1]) * query_unit
        from_state_ref[h] = grown * wide_query - product[:, :DK]
        own_ref[h] = product[:, DK:]


def make_readout(side, queries, keys, decays, solved):
    length = keys.shape[0]
    block = pl.BlockSpec((length, HALF * DK), lambda i, side: (0, side[0]))
    out = jax.ShapeDtypeStruct((HALF, length, DK), F32)
    own = jax.ShapeDtypeStruct((HALF, length, DV), F32)
    return pl.pallas_call(
        readout_kernel,
        out_shape=(out, own),
        grid_spec=pltpu.PrefetchScalarGridSpec(
            num_scalar_prefetch=1,
            grid=(1,),
            in_specs=[block, block, whole(decays.shape), whole(solved.shape)],
            out_specs=(whole(out.shape), whole(own.shape)),
        ),
        compiler_params=params(),
        name="readout_terms",
    )(side, queries, keys, decays, solved)


def finish_kernel(side_ref, from_state_ref, own_ref, state_ref, gate_ref, gain_ref, *rest):
    out_ref = rest[-1]
    gain = gain_ref[...]
    for h in range(HALF):
        readout = own_ref[h] + mul(from_state_ref[h], state_ref[h])
        mean = jnp.mean(readout * readout, axis=1, keepdims=True)
        gate = gate_ref[:, h * DV : (h + 1) * DV].astype(F32)
        scaled = readout * lax.rsqrt(mean + 1e-05) * gain
        gated = scaled * (gate / (1.0 + jnp.exp(-gate)))
        out_ref[:, h * DV : (h + 1) * DV] = gated.astype(BF16)


def finish(side, from_state, own, state, gate, gain, before=None):
    length = gate.shape[0]
    block = pl.BlockSpec((length, HALF * DV), lambda i, side: (0, side[0]))
    specs = [whole(from_state.shape), whole(own.shape), whole(state.shape), block, whole((1, DV))]
    operands = [side, from_state, own, state, gate, gain]
    aliases = {}
    if before is not None:
        specs.append(pl.BlockSpec(memory_space=pl.ANY))
        operands.append(before)
        aliases = {6: 0}
    return pl.pallas_call(
        finish_kernel,
        out_shape=jax.ShapeDtypeStruct(gate.shape, BF16),
        grid_spec=pltpu.PrefetchScalarGridSpec(
            num_scalar_prefetch=1, grid=(1,), in_specs=specs, out_specs=block
        ),
        input_output_aliases=aliases,
        compiler_params=params(),
        name="gated_readout",
    )(*operands)


def compose_into(later, earlier):
    both = mul(later[:, :DK], earlier)
    return both[:, :DK], both[:, DK:] + later[:, DK:]


def chip_kernel(place_ref, own_ref, other_ref, *out_refs):
    core, z = place_ref[0], place_ref[1]
    rounds = len(out_refs)
    share = HALF // rounds

    def go(first_ref, second_ref):
        for r, out_ref in enumerate(out_refs):
            base = (z ^ r) * share
            for i in range(share):
                a, b = compose_into(second_ref[base + i], first_ref[base + i])
                out_ref[i, :, :DK] = a
                out_ref[i, :, DK:] = b

    @pl.when(core == 0)
    def _():
        go(own_ref, other_ref)

    @pl.when(core != 0)
    def _():
        go(other_ref, own_ref)


def chip_maps(place, own, other, rounds):
    out = jax.ShapeDtypeStruct((HALF // rounds, DK, DK + DV), F32)
    return pl.pallas_call(
        chip_kernel,
        out_shape=(out,) * rounds,
        grid_spec=pltpu.PrefetchScalarGridSpec(
            num_scalar_prefetch=1,
            grid=(1,),
            in_specs=[whole(own.shape), whole(other.shape)],
            out_specs=(whole(out.shape),) * rounds,
        ),
        compiler_params=params(),
        name="chip_maps",
    )(place, own, other)


def group_kernel(place_ref, *refs):
    z = place_ref[1]
    rounds = len(refs) - 2
    in_refs, total_ref, prefix_ref = refs[:rounds], refs[rounds], refs[rounds + 1]
    share = total_ref.shape[0]
    for r, ref in enumerate(in_refs):
        prefix_ref[z ^ r] = ref[...]
    for i in range(share):
        running = prefix_ref[0, i]
        for k in range(1, rounds):
            later = prefix_ref[k, i]
            prefix_ref[k - 1, i] = running
            running = jnp.concatenate(compose_into(later, running), axis=1)
        total_ref[i] = running


def group_maps(place, pieces):
    shape = pieces[0].shape
    out = jax.ShapeDtypeStruct(shape, F32)
    prefix = jax.ShapeDtypeStruct((len(pieces),) + shape, F32)
    return pl.pallas_call(
        group_kernel,
        out_shape=(out, prefix),
        grid_spec=pltpu.PrefetchScalarGridSpec(
            num_scalar_prefetch=1,
            grid=(1,),
            in_specs=[whole(shape)] * len(pieces),
            out_specs=(whole(shape), whole(prefix.shape)),
        ),
        compiler_params=params(),
        name="group_maps",
    )(place, *pieces)


def state_kernel(place_ref, initial_ref, prefix_ref, *refs):
    z, group = place_ref[1], place_ref[2]
    rounds = prefix_ref.shape[0]
    scratch_ref = refs[-1]
    out_refs = refs[-1 - rounds : -1]
    in_refs = refs[: -1 - rounds]
    share = initial_ref.shape[0]
    for r, ref in enumerate(in_refs):
        scratch_ref[group ^ r] = ref[...]

    def advance(k, states):
        return tuple(
            mul(scratch_ref[k, i, :, :DK], states[i]) + scratch_ref[k, i, :, DK:]
            for i in range(share)
        )

    start = lax.fori_loop(0, group, advance, tuple(initial_ref[i] for i in range(share)))
    for r, out_ref in enumerate(out_refs):
        where = z ^ r
        back = jnp.maximum(where - 1, 0)
        for i in range(share):
            moved = mul(prefix_ref[back, i, :, :DK], start[i]) + prefix_ref[back, i, :, DK:]
            out_ref[i] = jnp.where(where == 0, start[i], moved)


def chip_states(place, initial, prefix, groups):
    rounds, share = prefix.shape[:2]
    out = jax.ShapeDtypeStruct((share, DK, DV), F32)
    piece = (share, DK, DK + DV)
    slots = HALF // share
    return pl.pallas_call(
        state_kernel,
        out_shape=(out,) * rounds,
        grid_spec=pltpu.PrefetchScalarGridSpec(
            num_scalar_prefetch=1,
            grid=(1,),
            in_specs=[
                pl.BlockSpec(
                    (share, DK, DV), lambda i, place: (place[0] * slots + place[1], 0, 0)
                ),
                whole(prefix.shape),
            ]
            + [whole(piece)] * len(groups),
            out_specs=(whole(out.shape),) * rounds,
            scratch_shapes=[pltpu.VMEM((len(groups),) + piece, F32)],
        ),
        compiler_params=params(),
        name="chip_states",
    )(place, initial, prefix, *groups)


def core_kernel(place_ref, own_ref, other_ref, *refs):
    core, z = place_ref[0], place_ref[1]
    keep_ref, give_ref = refs[-2:]
    in_refs = refs[:-2]
    share = in_refs[0].shape[0]

    def go(first_ref, start_ref, later_ref):
        for r, ref in enumerate(in_refs):
            base = (z ^ r) * share
            for i in range(share):
                state = ref[i]
                start_ref[base + i] = state
                later_ref[base + i] = (
                    mul(first_ref[base + i, :, :DK], state) + first_ref[base + i, :, DK:]
                )

    @pl.when(core == 0)
    def _():
        go(own_ref, keep_ref, give_ref)

    @pl.when(core != 0)
    def _():
        go(other_ref, give_ref, keep_ref)


def core_states(place, own, other, pieces):
    out = jax.ShapeDtypeStruct((HALF, DK, DV), F32)
    return pl.pallas_call(
        core_kernel,
        out_shape=(out, out),
        grid_spec=pltpu.PrefetchScalarGridSpec(
            num_scalar_prefetch=1,
            grid=(1,),
            in_specs=[whole(own.shape), whole(other.shape)]
            + [whole(pieces[0].shape)] * len(pieces),
            out_specs=(whole(out.shape), whole(out.shape)),
        ),
        compiler_params=params(),
        name="core_states",
    )(place, own, other, *pieces)


def matmul(left, right):
    return jnp.einsum("...ij,...jk->...ik", left, right, precision=HIGHEST)


def gathered_states(maps, initial):
    seq, grp = lax.axis_size("seq"), lax.axis_size("grp")
    place, group = lax.axis_index("seq"), lax.axis_index("grp")

    def compose(before, step):
        both = matmul(step[..., :DK], before)
        return both.at[..., DK:].add(step[..., DK:])

    heads = maps.shape[0]
    identity = jnp.concatenate(
        [jnp.eye(DK, dtype=F32), jnp.zeros((DK, DV), F32)], axis=1
    )
    identity = jnp.broadcast_to(identity, (heads, DK, DK + DV))
    everything = lax.all_gather(maps, "seq")

    def lap(k, carry):
        total, mine = carry
        mine = jnp.where(k == place, total, mine)
        return compose(total, everything[k]), mine

    total, mine = lax.fori_loop(0, seq, lap, (identity, identity))
    groups = lax.all_gather(total, "grp")

    def step(k, state):
        return matmul(groups[k][..., :DK], state) + groups[k][..., DK:]

    start = lax.fori_loop(0, group, step, initial)
    return matmul(mine[..., :DK], start) + mine[..., DK:]


def swap_pairs(size, bit):
    return [(i, i ^ bit) for i in range(size)]


def body(
    query_proj, key_proj, value_proj, log_decay, write_rate, gate_proj, norm_gain, initial_state
):
    seq, grp = lax.axis_size("seq"), lax.axis_size("grp")
    chips = seq // 2
    place = lax.axis_index("seq")
    core, z, group = place % 2, place // 2, lax.axis_index("grp")
    gain = norm_gain.reshape(1, DV)
    mine = core.reshape(1).astype(jnp.int32)
    theirs = 1 - mine
    fast = seq % 2 == 0 and chips in (1, 2, 4, 8) and grp & (grp - 1) == 0

    maps_theirs, solved_theirs = make_maps(theirs, key_proj, value_proj, log_decay, write_rate)
    if not fast:
        maps_mine, solved_mine = make_maps(mine, key_proj, value_proj, log_decay, write_rate)
        maps = jnp.where(
            core == 0,
            jnp.concatenate([maps_mine, maps_theirs]),
            jnp.concatenate([maps_theirs, maps_mine]),
        )
        state = gathered_states(maps, initial_state)
        state_mine = lax.dynamic_slice_in_dim(state, core * HALF, HALF)
        state_theirs = lax.dynamic_slice_in_dim(state, (1 - core) * HALF, HALF)
        terms_mine = make_readout(mine, query_proj, key_proj, log_decay, solved_mine)
        terms_theirs = make_readout(theirs, query_proj, key_proj, log_decay, solved_theirs)
    else:
        spot = jnp.stack([core, z, group]).astype(jnp.int32)
        other = lax.ppermute(maps_theirs, "seq", swap_pairs(seq, 1))
        maps_mine, solved_mine = make_maps(mine, key_proj, value_proj, log_decay, write_rate)
        chip = chip_maps(spot, maps_mine, other, chips)
        pieces = [chip[0]] + [
            lax.ppermute(chip[r], "seq", swap_pairs(seq, 2 * r)) for r in range(1, chips)
        ]
        terms_mine = make_readout(mine, query_proj, key_proj, log_decay, solved_mine)
        terms_theirs = make_readout(theirs, query_proj, key_proj, log_decay, solved_theirs)
        total, prefix = group_maps(spot, pieces)
        groups = [total] + [
            lax.ppermute(total, "grp", swap_pairs(grp, r)) for r in range(1, grp)
        ]
        starts = chip_states(spot, initial_state, prefix, groups)
        back = [starts[0]] + [
            lax.ppermute(starts[r], "seq", swap_pairs(seq, 2 * r)) for r in range(1, chips)
        ]
        state_mine, give = core_states(spot, maps_mine, other, back)
        state_theirs = lax.ppermute(give, "seq", swap_pairs(seq, 1))

    out = finish(mine, *terms_mine, state_mine, gate_proj, gain)
    return finish(theirs, *terms_theirs, state_theirs, gate_proj, gain, out)


def solution(mesh):
    spread = P(("grp", "seq"), None)
    placed = (spread,) * 6 + (P(), P())
    return jax.shard_map(body, mesh=mesh, in_specs=placed, out_specs=spread, check_vma=False)
```

```python
import functools

import jax
import jax.numpy as jnp
from jax import lax
from jax.experimental import pallas as pl
from jax.experimental.pallas import tpu as pltpu
from jax.sharding import PartitionSpec as P

ATTENTION_UNITS = 16
DK = 128
DV = 128
HALF = ATTENTION_UNITS // 2
F32 = jnp.float32
BF16 = jnp.bfloat16
HIGHEST = lax.Precision.HIGHEST
VMEM_LIMIT = 8 * 1024 * 1024
VMEM_ALL = 8 * 1024 * 1024
VECTOR = pl.BlockSpec(memory_space=pltpu.VMEM)
SCALAR = pl.BlockSpec(memory_space=pltpu.SMEM)
ANYWHERE = pl.BlockSpec(memory_space=pl.ANY)
DISTANT = pl.BlockSpec(memory_space=pltpu.HBM)


def dot(left, right):
    return jnp.dot(left, right, preferred_element_type=F32)


def dot_t(left, right):
    return lax.dot_general(left, right, (((1,), (1,)), ((), ())), preferred_element_type=F32)


def t_dot(left, right):
    return lax.dot_general(left, right, (((0,), (0,)), ((), ())), preferred_element_type=F32)


def split(x):
    high = x.astype(BF16)
    low = (x - high.astype(F32)).astype(BF16)
    return high, low


def wide(x):
    return jnp.concatenate(split(x), axis=1)


def halves_sum(x):
    width = x.shape[1] // 2
    return x[:, :width] + x[:, width:]


def mul(left, right):
    pair = wide(left)
    high, low = split(right)
    if right.shape[1] == DK:
        row = jnp.concatenate([high, low], axis=1)
        return halves_sum(dot(pair, jnp.concatenate([row, row], axis=0)))
    return dot(pair, jnp.concatenate([high, high], axis=0)) + dot(
        pair, jnp.concatenate([low, low], axis=0)
    )


def mul_exact(left, right):
    return dot(wide(left), jnp.concatenate([right, right], axis=0))


def positions(size):
    later = lax.broadcasted_iota(jnp.int32, (size, size), 0)
    earlier = lax.broadcasted_iota(jnp.int32, (size, size), 1)
    return later, earlier


def three(x):
    first = x.astype(BF16)
    rest = x - first.astype(F32)
    second = rest.astype(BF16)
    third = (rest - second.astype(F32)).astype(BF16)
    return first, second, third


def running_sum(decay_rows):
    earlier, later = positions(decay_rows.shape[1])
    ones = jnp.where(earlier <= later, 1.0, 0.0).astype(BF16)
    first, second, third = three(decay_rows)
    return dot(first, ones) + (dot(second, ones) + dot(third, ones))


def pick(x, side, start, count):
    low = x[start : start + count]
    high = x[HALF + start : HALF + start + count]
    return jnp.where(side == 0, low, high)


def lanes(ref, side, start, h):
    offset = pl.multiple_of((side * HALF + start + h) * DK, DK)
    return ref[:, pl.ds(offset, DK)]


def call(kernel, name, operands, specs, out_shape, out_specs=None, scratch=(), limit=None):
    return pl.pallas_call(
        kernel,
        out_shape=out_shape,
        in_specs=specs,
        out_specs=out_specs or jax.tree.map(lambda _: VECTOR, out_shape),
        scratch_shapes=scratch,
        compiler_params=pltpu.CompilerParams(vmem_limit_bytes=limit or VMEM_LIMIT),
        name=name,
    )(*operands)


def fetch(pairs, arrived):
    copies = [
        pltpu.make_async_copy(source, target, arrived.at[k])
        for k, (source, target) in enumerate(pairs)
    ]
    for copy in copies:
        copy.start()
    return copies


def shaped(*shape):
    return jax.ShapeDtypeStruct(shape, F32)


def staged_map_kernel(start, count, side_ref, key_ref, value_ref, decay_ref, rate_ref, *refs):
    maps_ref, inverse_ref, key_here, value_here, decay_here, rate_here, arrived = refs[-7:]
    offset = pl.multiple_of((side_ref[0] * HALF + start) * DK, DK)
    window = (slice(None), pl.ds(offset, count * DK))
    pairs = (
        (key_ref.at[window], key_here),
        (decay_ref, decay_here),
        (rate_ref, rate_here),
        (value_ref.at[window], value_here),
    )
    for copy in fetch(pairs, arrived):
        copy.wait()
    map_work(
        start,
        count,
        side_ref[0],
        [key_here[:, h * DK : (h + 1) * DK] for h in range(count)],
        [value_here[:, h * DV : (h + 1) * DV] for h in range(count)],
        decay_here[...],
        rate_here[...],
        maps_ref,
        inverse_ref,
    )


def map_kernel(start, count, side_ref, key_ref, value_ref, decay_ref, rate_ref, *refs):
    side = side_ref[0]
    map_work(
        start,
        count,
        side,
        [lanes(key_ref, side, start, h) for h in range(count)],
        [lanes(value_ref, side, start, h) for h in range(count)],
        decay_ref[...],
        rate_ref[...],
        *refs[-2:],
    )


def map_work(start, count, side, keys, values, decays, rates, maps_ref, inverse_ref):
    length = keys[0].shape[0]
    later, earlier = positions(length)
    eye = later == earlier
    strict = later > earlier
    identity = jnp.where(eye, 1.0, 0.0)
    total_row = pick(running_sum(decays), side, start, count)
    rate_row = pick(rates, side, start, count)
    total_col, rate_col = total_row.T, rate_row.T
    heads = range(count)
    grams = [dot_t(keys[h], keys[h]) for h in heads]
    lower, unit_row, unit_col = [], [], []
    for h in heads:
        diagonal = jnp.where(eye, grams[h], 0.0)
        row = lax.rsqrt(jnp.sum(diagonal, axis=0, keepdims=True) + 1e-06)
        col = lax.rsqrt(jnp.sum(diagonal, axis=1, keepdims=True) + 1e-06)
        spread = total_col[:, h : h + 1] - total_row[h : h + 1, :]
        damping = jnp.exp(jnp.where(strict, spread, 0.0))
        scale = (rate_col[:, h : h + 1] * col) * row
        lower.append(jnp.where(strict, grams[h] * scale * damping, 0.0))
        unit_row.append(row)
        unit_col.append(col)
    inverse = [
        identity - jnp.where((later // 2) == (earlier // 2), lower[h], 0.0) for h in heads
    ]
    size = 2
    while size < length:
        band = ((later // (2 * size)) == (earlier // (2 * size))) & (
            (later // size) != (earlier // size)
        )
        inner = [mul(jnp.where(band, lower[h], 0.0), inverse[h]) for h in heads]
        outer = [mul(inverse[h], inner[h]) for h in heads]
        inverse = [inverse[h] - outer[h] for h in heads]
        size *= 2
    for h in heads:
        inverse_ref[h] = inverse[h]
    for h in heads:
        row = total_row[h : h + 1, :]
        rate = rate_row[h : h + 1, :]
        erase = mul_exact(inverse[h] * (rate * jnp.exp(row) * unit_row[h]), keys[h])
        insert = mul_exact(inverse[h] * rate, values[h])
        solved = jnp.concatenate([erase, insert], axis=1)
        final = total_col[length - 1 : length, h : h + 1]
        carried = jnp.exp(final - total_col[:, h : h + 1]) * unit_col[h]
        high, low = split(solved * carried)
        moved = t_dot(keys[h], high) + t_dot(keys[h], low)
        maps_ref[h, :, :DK] = jnp.exp(final) * identity - moved[:, :DK]
        maps_ref[h, :, DK:] = moved[:, DK:]


def make_maps(side, start, count, keys, values, decays, rates, after=(), scalars=None):
    length = keys.shape[0]
    first = scalars is not None
    scratch = []
    if first:
        scratch = [
            pltpu.VMEM((length, count * DK), BF16),
            pltpu.VMEM((length, count * DV), BF16),
            pltpu.VMEM(decays.shape, F32),
            pltpu.VMEM(rates.shape, F32),
            pltpu.SemaphoreType.DMA((4,)),
        ]
    scalars = list(scalars or ())
    return call(
        functools.partial(staged_map_kernel if first else map_kernel, start, count),
        "block_maps",
        [side, keys, values, decays, rates, *scalars, *after],
        [SCALAR]
        + [DISTANT if first else VECTOR] * 4
        + [SCALAR] * len(scalars)
        + [ANYWHERE] * len(after),
        (shaped(count, DK, DK + DV), shaped(count, length, length)),
        scratch=scratch,
        limit=VMEM_ALL if first else None,
    )


def readout_kernel(start, count, side_ref, *refs):
    queries, keys, values, decays, rates, inverse = refs[:6]
    from_state, own = refs[-2:]
    side = side_ref[0]
    length = queries.shape[0]
    later, earlier = positions(length)
    within = later >= earlier
    total_row = pick(running_sum(decays[...]), side, start, count)
    rate_row = pick(rates[...], side, start, count)
    total_col = total_row.T
    for h in range(count):
        query, key, value = (lanes(ref, side, start, h) for ref in (queries, keys, values))
        wide_query = query.astype(F32)
        wide_key = key.astype(F32)
        query_unit = lax.rsqrt(jnp.sum(wide_query * wide_query, axis=1, keepdims=True) + 1e-06)
        key_unit = lax.rsqrt(jnp.sum(wide_key * wide_key, axis=1, keepdims=True) + 1e-06)
        key_row = jnp.broadcast_to(key_unit, (length, DK)).T[:1, :]
        row, rate = total_row[h : h + 1, :], rate_row[h : h + 1, :]
        damping = jnp.exp(jnp.where(within, total_col[:, h : h + 1] - row, 0.0))
        mix = jnp.where(within, dot_t(query, key) * damping * query_unit * key_row, 0.0)
        product = mul(mix, inverse[h])
        grown = jnp.exp(total_col[:, h : h + 1]) * query_unit
        erased = mul_exact(product * (rate * jnp.exp(row) * key_row), key)
        from_state[h] = grown * wide_query - erased
        own[h] = mul_exact(product * rate, value)


def make_readout(side, start, count, queries, keys, values, decays, rates, inverse, after=()):
    length = keys.shape[0]
    return call(
        functools.partial(readout_kernel, start, count),
        "readout_terms",
        [side, queries, keys, values, decays, rates, inverse, *after],
        [SCALAR] + [VECTOR] * 6 + [ANYWHERE] * len(after),
        (shaped(count, length, DK), shaped(count, length, DV)),
    )


def finish_kernel(count, block_ref, from_state_ref, own_ref, state_ref, gate_ref, gain_ref, *refs):
    out_ref = refs[-1]
    gain = gain_ref[...]
    for h in range(count):
        readout = own_ref[h] + mul(from_state_ref[h], state_ref[h])
        mean = jnp.mean(readout * readout, axis=1, keepdims=True)
        gate = gate_ref[:, h * DV : (h + 1) * DV].astype(F32)
        scaled = readout * lax.rsqrt(mean + 1e-05) * gain
        gated = scaled * (gate / (1.0 + jnp.exp(-gate)))
        out_ref[:, h * DV : (h + 1) * DV] = gated.astype(BF16)


def finish(side, start, count, from_state, own, state, gate, gain, before, after=()):
    parts = HALF // count
    block = pl.BlockSpec(
        (gate.shape[0], count * DV), lambda i, side: (0, side[0] * parts + start // count)
    )

    def whole(x):
        return pl.BlockSpec(x.shape, lambda i, where: (0,) * x.ndim)

    extra = ([] if before is None else [before]) + list(after)
    return pl.pallas_call(
        functools.partial(finish_kernel, count),
        out_shape=jax.ShapeDtypeStruct(gate.shape, BF16),
        grid_spec=pltpu.PrefetchScalarGridSpec(
            num_scalar_prefetch=1,
            grid=(1,),
            in_specs=[whole(from_state), whole(own), whole(state), block, whole(gain)]
            + [ANYWHERE] * len(extra),
            out_specs=block,
        ),
        input_output_aliases={} if before is None else {6: 0},
        compiler_params=pltpu.CompilerParams(vmem_limit_bytes=VMEM_LIMIT),
        name="gated_readout",
    )(side, from_state, own, state, gate, gain, *extra)


def compose_into(later, earlier):
    both = mul(later[:, :DK], earlier)
    return both[:, :DK], both[:, DK:] + later[:, DK:]


def chip_kernel(core_ref, z_ref, own_ref, other_ref, *refs):
    z = z_ref[0]
    count = own_ref.shape[0]
    first_out, out_refs = refs[-1 - count], refs[-count:]

    def go(first_ref, second_ref):
        for r, out_ref in enumerate(out_refs):
            a, b = compose_into(second_ref[z ^ r], first_ref[z ^ r])
            out_ref[:, :DK] = a
            out_ref[:, DK:] = b
        first_out[...] = first_ref[...]

    @pl.when(core_ref[0] == 0)
    def _():
        go(own_ref, other_ref)

    @pl.when(core_ref[0] != 0)
    def _():
        go(other_ref, own_ref)


def chip_maps(core, z, own, other, after=()):
    return call(
        chip_kernel,
        "chip_maps",
        [core, z, own, other, *after],
        [SCALAR, SCALAR, VECTOR, VECTOR] + [ANYWHERE] * len(after),
        (shaped(*own.shape),) + (shaped(DK, DK + DV),) * own.shape[0],
    )


def group_kernel(rounds, z_ref, *refs):
    z = z_ref[0]
    in_refs = refs[:rounds]
    total_ref, prefix_ref, ordered_ref = refs[-3:]
    for r in range(rounds):
        ordered_ref[z ^ r] = in_refs[r][...]
    running = ordered_ref[0]
    for k in range(1, rounds):
        prefix_ref[k - 1] = running
        a, b = compose_into(ordered_ref[k], running)
        running = jnp.concatenate([a, b], axis=1)
    total_ref[...] = running


def group_maps(z, pieces, after=()):
    rounds = len(pieces)
    return call(
        functools.partial(group_kernel, rounds),
        "group_maps",
        [z, *pieces, *after],
        [SCALAR] + [VECTOR] * rounds + [ANYWHERE] * len(after),
        (shaped(DK, DK + DV), shaped(rounds - 1, DK, DK + DV)),
        scratch=[pltpu.VMEM((rounds, DK, DK + DV), F32)],
    )


def state_kernel(
    start, count, groups, core_ref, z_ref, group_ref, initial_ref, prefix_ref, *refs
):
    z, group = z_ref[0], group_ref[0]
    ordered_ref = refs[-1]
    out_refs = refs[-1 - count : -1]
    in_refs = refs[:groups]
    for r, ref in enumerate(in_refs):
        ordered_ref[group ^ r] = ref[...]

    def advance(k, state):
        return mul(ordered_ref[k, :, :DK], state) + ordered_ref[k, :, DK:]

    state = lax.fori_loop(0, group, advance, initial_ref[core_ref[0] * HALF + start + z])
    for r, out_ref in enumerate(out_refs):
        spot = z ^ r
        back = jnp.maximum(spot - 1, 0)
        moved = mul(prefix_ref[back, :, :DK], state) + prefix_ref[back, :, DK:]
        out_ref[...] = jnp.where(spot == 0, state, moved)


def chip_states(start, count, core, z, group, initial, prefix, groups, after=()):
    return call(
        functools.partial(state_kernel, start, count, len(groups)),
        "chip_states",
        [core, z, group, initial, prefix, *groups, *after],
        [SCALAR] * 3 + [VECTOR] * (2 + len(groups)) + [ANYWHERE] * len(after),
        (shaped(DK, DV),) * count,
        scratch=[
            pltpu.VMEM((len(groups), DK, DK + DV), F32),
        ],
    )


def core_kernel(core_ref, z_ref, first_ref, *refs):
    z = z_ref[0]
    count = first_ref.shape[0]
    in_refs = refs[:count]
    keep_ref, give_ref = refs[-2:]

    def go(start_ref, later_ref):
        for r, ref in enumerate(in_refs):
            state = ref[...]
            start_ref[z ^ r] = state
            later_ref[z ^ r] = mul(first_ref[z ^ r, :, :DK], state) + first_ref[z ^ r, :, DK:]

    @pl.when(core_ref[0] == 0)
    def _():
        go(keep_ref, give_ref)

    @pl.when(core_ref[0] != 0)
    def _():
        go(give_ref, keep_ref)


def core_states(core, z, first, pieces, after=()):
    out = shaped(len(pieces), DK, DV)
    return call(
        core_kernel,
        "core_states",
        [core, z, first, *pieces, *after],
        [SCALAR] * 2 + [VECTOR] * (1 + len(pieces)) + [ANYWHERE] * len(after),
        (out, out),
    )


def matmul(left, right):
    return jnp.einsum("...ij,...jk->...ik", left, right, precision=HIGHEST)


def gathered_states(maps, initial):
    seq, grp = lax.axis_size("seq"), lax.axis_size("grp")
    place, group = lax.axis_index("seq"), lax.axis_index("grp")

    def compose(before, step):
        both = matmul(step[..., :DK], before)
        return both.at[..., DK:].add(step[..., DK:])

    heads = maps.shape[0]
    identity = jnp.concatenate(
        [jnp.eye(DK, dtype=F32), jnp.zeros((DK, DV), F32)], axis=1
    )
    identity = jnp.broadcast_to(identity, (heads, DK, DK + DV))
    everything = lax.all_gather(maps, "seq")

    def lap(k, carry):
        total, mine = carry
        mine = jnp.where(k == place, total, mine)
        return compose(total, everything[k]), mine

    total, mine = lax.fori_loop(0, seq, lap, (identity, identity))
    groups = lax.all_gather(total, "grp")

    def step(k, state):
        return matmul(groups[k][..., :DK], state) + groups[k][..., DK:]

    start = lax.fori_loop(0, group, step, initial)
    return matmul(mine[..., :DK], start) + mine[..., DK:]


def swap_pairs(size, bit):
    return [(i, i ^ bit) for i in range(size)]


def body(
    query_proj, key_proj, value_proj, log_decay, write_rate, gate_proj, norm_gain, initial_state
):
    seq, grp = lax.axis_size("seq"), lax.axis_size("grp")
    chips = seq // 2
    place = lax.axis_index("seq")
    group = lax.axis_index("grp").astype(jnp.int32).reshape(1)
    core, z = (place % 2).astype(jnp.int32).reshape(1), (place // 2).astype(jnp.int32).reshape(1)
    gain = norm_gain.reshape(1, DV)
    mine, theirs = core, 1 - core
    decays, rates = log_decay.T, write_rate.T
    fast = seq % 2 == 0 and chips in (2, 4, 8) and grp & (grp - 1) == 0

    def maps_of(side, start, count, **options):
        return make_maps(side, start, count, key_proj, value_proj, decays, rates, **options)

    def terms_of(side, start, count, inverse, after=()):
        return make_readout(
            side, start, count, query_proj, key_proj, value_proj, decays, rates, inverse, after
        )

    out = None
    if not fast:
        maps_mine, solved_mine = maps_of(mine, 0, HALF)
        maps_theirs, solved_theirs = maps_of(theirs, 0, HALF)
        maps = jnp.where(
            core[0] == 0,
            jnp.concatenate([maps_mine, maps_theirs]),
            jnp.concatenate([maps_theirs, maps_mine]),
        )
        state = gathered_states(maps, initial_state)
        for side, solved in ((mine, solved_mine), (theirs, solved_theirs)):
            part = lax.dynamic_slice_in_dim(state, side[0] * HALF, HALF)
            terms = terms_of(side, 0, HALF, solved)
            out = finish(side, 0, HALF, *terms, part, gate_proj, gain, out)
        return out

    starts = range(0, HALF, chips)
    firsts, inverses, pieces, terms, after = [], [], [], [], ()
    for k, start in enumerate(starts):
        scalars = (mine, z, group) if k == 0 else None
        maps_theirs, inverse_theirs = maps_of(theirs, start, chips, after=after, scalars=scalars)
        other = lax.ppermute(maps_theirs, "seq", swap_pairs(seq, 1))
        maps_mine, inverse_mine = maps_of(mine, start, chips, after=(inverse_theirs,))
        inverses += [(mine, start, inverse_mine), (theirs, start, inverse_theirs)]
        first, *chip = chip_maps(core, z, maps_mine, other)
        firsts.append(first)
        after = (chip[0],)
        pieces.append(
            [chip[0]]
            + [lax.ppermute(chip[r], "seq", swap_pairs(seq, 2 * r)) for r in range(1, chips)]
        )
    prefixes, groups = [], []
    for k, start in enumerate(starts):
        total, prefix = group_maps(z, pieces[k], after)
        prefixes.append(prefix)
        groups.append(
            [total] + [lax.ppermute(total, "grp", swap_pairs(grp, r)) for r in range(1, grp)]
        )
        after = (total,)
        if k == 0:
            for side, begin, inverse in inverses:
                terms.append(terms_of(side, begin, chips, inverse, after))
                after = (terms[-1][0],)
    backs = []
    for k, start in enumerate(starts):
        back = chip_states(
            start, chips, core, z, group, initial_state, prefixes[k], groups[k], after
        )
        after = (back[0],)
        backs.append(
            [back[0]]
            + [lax.ppermute(back[r], "seq", swap_pairs(seq, 2 * r)) for r in range(1, chips)]
        )
    states = []
    for k, start in enumerate(starts):
        state, give = core_states(core, z, firsts[k], backs[k], after)
        after = (state,)
        states.append((state, lax.ppermute(give, "seq", swap_pairs(seq, 1))))
    for k, start in enumerate(starts):
        for part, side in enumerate((mine, theirs)):
            out = finish(
                side, start, chips, *terms[2 * k + part], states[k][part], gate_proj, gain, out, after
            )
            after = ()
    return out


def solution(mesh):
    spread = P(("grp", "seq"), None)
    placed = (spread,) * 6 + (P(), P())
    return jax.shard_map(body, mesh=mesh, in_specs=placed, out_specs=spread, check_vma=False)
```

```python
import functools

import jax
import jax.numpy as jnp
from jax import lax
from jax.experimental import pallas as pl
from jax.experimental.pallas import tpu as pltpu
from jax.sharding import PartitionSpec as P

ATTENTION_UNITS = 16
DK = 128
DV = 128
HALF = ATTENTION_UNITS // 2
F32 = jnp.float32
BF16 = jnp.bfloat16
HIGHEST = lax.Precision.HIGHEST
VMEM_LIMIT = 8 * 1024 * 1024
VMEM_ALL = 8 * 1024 * 1024
VECTOR = pl.BlockSpec(memory_space=pltpu.VMEM)
SCALAR = pl.BlockSpec(memory_space=pltpu.SMEM)
ANYWHERE = pl.BlockSpec(memory_space=pl.ANY)
DISTANT = pl.BlockSpec(memory_space=pltpu.HBM)


def dot(left, right):
    return jnp.dot(left, right, preferred_element_type=F32)


def dot_t(left, right):
    return lax.dot_general(left, right, (((1,), (1,)), ((), ())), preferred_element_type=F32)


def t_dot(left, right):
    return lax.dot_general(left, right, (((0,), (0,)), ((), ())), preferred_element_type=F32)


def split(x):
    high = x.astype(BF16)
    low = (x - high.astype(F32)).astype(BF16)
    return high, low


def wide(x):
    return jnp.concatenate(split(x), axis=1)


def halves_sum(x):
    width = x.shape[1] // 2
    return x[:, :width] + x[:, width:]


def mul(left, right):
    pair = wide(left)
    high, low = split(right)
    if right.shape[1] == DK:
        row = jnp.concatenate([high, low], axis=1)
        return halves_sum(dot(pair, jnp.concatenate([row, row], axis=0)))
    return dot(pair, jnp.concatenate([high, high], axis=0)) + dot(
        pair, jnp.concatenate([low, low], axis=0)
    )


def mul_exact(left, right):
    return dot(wide(left), jnp.concatenate([right, right], axis=0))


def positions(size):
    later = lax.broadcasted_iota(jnp.int32, (size, size), 0)
    earlier = lax.broadcasted_iota(jnp.int32, (size, size), 1)
    return later, earlier


def three(x):
    first = x.astype(BF16)
    rest = x - first.astype(F32)
    second = rest.astype(BF16)
    third = (rest - second.astype(F32)).astype(BF16)
    return first, second, third


def running_sum(decay_rows):
    earlier, later = positions(decay_rows.shape[1])
    ones = jnp.where(earlier <= later, 1.0, 0.0).astype(BF16)
    first, second, third = three(decay_rows)
    return dot(first, ones) + (dot(second, ones) + dot(third, ones))


def pick(x, side, start, count):
    low = x[start : start + count]
    high = x[HALF + start : HALF + start + count]
    return jnp.where(side == 0, low, high)


def lanes(ref, side, start, h):
    offset = pl.multiple_of((side * HALF + start + h) * DK, DK)
    return ref[:, pl.ds(offset, DK)]


def call(kernel, name, operands, specs, out_shape, out_specs=None, scratch=(), limit=None):
    return pl.pallas_call(
        kernel,
        out_shape=out_shape,
        in_specs=specs,
        out_specs=out_specs or jax.tree.map(lambda _: VECTOR, out_shape),
        scratch_shapes=scratch,
        compiler_params=pltpu.CompilerParams(vmem_limit_bytes=limit or VMEM_LIMIT),
        name=name,
    )(*operands)


def fetch(pairs, arrived):
    copies = [
        pltpu.make_async_copy(source, target, arrived.at[k])
        for k, (source, target) in enumerate(pairs)
    ]
    for copy in copies:
        copy.start()
    return copies


def shaped(*shape):
    return jax.ShapeDtypeStruct(shape, F32)


def staged_map_kernel(start, count, side_ref, key_ref, value_ref, decay_ref, rate_ref, *refs):
    maps_ref, inverse_ref, key_here, value_here, decay_here, rate_here, arrived = refs[-7:]
    offset = pl.multiple_of((side_ref[0] * HALF + start) * DK, DK)
    window = (slice(None), pl.ds(offset, count * DK))
    pairs = (
        (key_ref.at[window], key_here),
        (decay_ref, decay_here),
        (rate_ref, rate_here),
        (value_ref.at[window], value_here),
    )
    key_copy, decay_copy, rate_copy, value_copy = fetch(pairs, arrived)
    decay_copy.wait()
    rate_copy.wait()
    key_copy.wait()

    def values():
        value_copy.wait()
        return [value_here[:, h * DV : (h + 1) * DV] for h in range(count)]

    map_work(
        start,
        count,
        side_ref[0],
        [key_here[:, h * DK : (h + 1) * DK] for h in range(count)],
        values,
        decay_here[...],
        rate_here[...],
        maps_ref,
        inverse_ref,
    )


def map_kernel(start, count, side_ref, key_ref, value_ref, decay_ref, rate_ref, *refs):
    side = side_ref[0]
    map_work(
        start,
        count,
        side,
        [lanes(key_ref, side, start, h) for h in range(count)],
        lambda: [lanes(value_ref, side, start, h) for h in range(count)],
        decay_ref[...],
        rate_ref[...],
        *refs[-2:],
    )


def map_work(start, count, side, keys, values, decays, rates, maps_ref, inverse_ref):
    length = keys[0].shape[0]
    later, earlier = positions(length)
    eye = later == earlier
    strict = later > earlier
    identity = jnp.where(eye, 1.0, 0.0)
    total_row = pick(running_sum(decays), side, start, count)
    rate_row = pick(rates, side, start, count)
    total_col, rate_col = total_row.T, rate_row.T
    heads = range(count)
    grams = [dot_t(keys[h], keys[h]) for h in heads]
    lower, unit_row, unit_col = [], [], []
    for h in heads:
        diagonal = jnp.where(eye, grams[h], 0.0)
        row = lax.rsqrt(jnp.sum(diagonal, axis=0, keepdims=True) + 1e-06)
        col = lax.rsqrt(jnp.sum(diagonal, axis=1, keepdims=True) + 1e-06)
        spread = total_col[:, h : h + 1] - total_row[h : h + 1, :]
        damping = jnp.exp(jnp.where(strict, spread, 0.0))
        scale = (rate_col[:, h : h + 1] * col) * row
        lower.append(jnp.where(strict, grams[h] * scale * damping, 0.0))
        unit_row.append(row)
        unit_col.append(col)
    inverse = [
        identity - jnp.where((later // 2) == (earlier // 2), lower[h], 0.0) for h in heads
    ]
    size = 2
    while size < length:
        band = ((later // (2 * size)) == (earlier // (2 * size))) & (
            (later // size) != (earlier // size)
        )
        inner = [mul(jnp.where(band, lower[h], 0.0), inverse[h]) for h in heads]
        outer = [mul(inverse[h], inner[h]) for h in heads]
        inverse = [inverse[h] - outer[h] for h in heads]
        size *= 2
    for h in heads:
        inverse_ref[h] = inverse[h]
    values = values()
    for h in heads:
        row = total_row[h : h + 1, :]
        rate = rate_row[h : h + 1, :]
        erase = mul_exact(inverse[h] * (rate * jnp.exp(row) * unit_row[h]), keys[h])
        insert = mul_exact(inverse[h] * rate, values[h])
        solved = jnp.concatenate([erase, insert], axis=1)
        final = total_col[length - 1 : length, h : h + 1]
        carried = jnp.exp(final - total_col[:, h : h + 1]) * unit_col[h]
        high, low = split(solved * carried)
        moved = t_dot(keys[h], high) + t_dot(keys[h], low)
        maps_ref[h, :, :DK] = jnp.exp(final) * identity - moved[:, :DK]
        maps_ref[h, :, DK:] = moved[:, DK:]


def make_maps(side, start, count, keys, values, decays, rates, after=(), scalars=None):
    length = keys.shape[0]
    first = scalars is not None
    scratch = []
    if first:
        scratch = [
            pltpu.VMEM((length, count * DK), BF16),
            pltpu.VMEM((length, count * DV), BF16),
            pltpu.VMEM(decays.shape, F32),
            pltpu.VMEM(rates.shape, F32),
            pltpu.SemaphoreType.DMA((4,)),
        ]
        keys, values = (pltpu.with_memory_space_constraint(x, pltpu.HBM) for x in (keys, values))
    scalars = list(scalars or ())
    return call(
        functools.partial(staged_map_kernel if first else map_kernel, start, count),
        "block_maps",
        [side, keys, values, decays, rates, *scalars, *after],
        [SCALAR]
        + [DISTANT if first else VECTOR] * 4
        + [SCALAR] * len(scalars)
        + [ANYWHERE] * len(after),
        (shaped(count, DK, DK + DV), shaped(count, length, length)),
        scratch=scratch,
        limit=VMEM_ALL if first else None,
    )


def readout_kernel(start, count, side_ref, *refs):
    queries, keys, values, decays, rates, inverse = refs[:6]
    from_state, own = refs[-2:]
    side = side_ref[0]
    length = queries.shape[0]
    later, earlier = positions(length)
    within = later >= earlier
    total_row = pick(running_sum(decays[...]), side, start, count)
    rate_row = pick(rates[...], side, start, count)
    total_col = total_row.T
    for h in range(count):
        query, key, value = (lanes(ref, side, start, h) for ref in (queries, keys, values))
        wide_query = query.astype(F32)
        wide_key = key.astype(F32)
        query_unit = lax.rsqrt(jnp.sum(wide_query * wide_query, axis=1, keepdims=True) + 1e-06)
        key_unit = lax.rsqrt(jnp.sum(wide_key * wide_key, axis=1, keepdims=True) + 1e-06)
        key_row = jnp.broadcast_to(key_unit, (length, DK)).T[:1, :]
        row, rate = total_row[h : h + 1, :], rate_row[h : h + 1, :]
        damping = jnp.exp(jnp.where(within, total_col[:, h : h + 1] - row, 0.0))
        mix = jnp.where(within, dot_t(query, key) * damping * query_unit * key_row, 0.0)
        product = mul(mix, inverse[h])
        grown = jnp.exp(total_col[:, h : h + 1]) * query_unit
        erased = mul_exact(product * (rate * jnp.exp(row) * key_row), key)
        from_state[h] = grown * wide_query - erased
        own[h] = mul_exact(product * rate, value)


def make_readout(side, start, count, queries, keys, values, decays, rates, inverse, after=()):
    length = keys.shape[0]
    return call(
        functools.partial(readout_kernel, start, count),
        "readout_terms",
        [side, queries, keys, values, decays, rates, inverse, *after],
        [SCALAR] + [VECTOR] * 6 + [ANYWHERE] * len(after),
        (shaped(count, length, DK), shaped(count, length, DV)),
    )


def finish_kernel(count, block_ref, from_state_ref, own_ref, state_ref, gate_ref, gain_ref, *refs):
    out_ref = refs[-1]
    gain = gain_ref[...]
    for h in range(count):
        readout = own_ref[h] + mul(from_state_ref[h], state_ref[h])
        mean = jnp.mean(readout * readout, axis=1, keepdims=True)
        gate = gate_ref[:, h * DV : (h + 1) * DV].astype(F32)
        scaled = readout * lax.rsqrt(mean + 1e-05) * gain
        gated = scaled * (gate / (1.0 + jnp.exp(-gate)))
        out_ref[:, h * DV : (h + 1) * DV] = gated.astype(BF16)


def finish(side, start, count, from_state, own, state, gate, gain, before, after=()):
    parts = HALF // count
    block = pl.BlockSpec(
        (gate.shape[0], count * DV), lambda i, side: (0, side[0] * parts + start // count)
    )

    def whole(x):
        return pl.BlockSpec(x.shape, lambda i, where: (0,) * x.ndim)

    extra = ([] if before is None else [before]) + list(after)
    return pl.pallas_call(
        functools.partial(finish_kernel, count),
        out_shape=jax.ShapeDtypeStruct(gate.shape, BF16),
        grid_spec=pltpu.PrefetchScalarGridSpec(
            num_scalar_prefetch=1,
            grid=(1,),
            in_specs=[whole(from_state), whole(own), whole(state), block, whole(gain)]
            + [ANYWHERE] * len(extra),
            out_specs=block,
        ),
        input_output_aliases={} if before is None else {6: 0},
        compiler_params=pltpu.CompilerParams(vmem_limit_bytes=VMEM_LIMIT),
        name="gated_readout",
    )(side, from_state, own, state, gate, gain, *extra)


def compose_into(later, earlier):
    both = mul(later[:, :DK], earlier)
    return both[:, :DK], both[:, DK:] + later[:, DK:]


def chip_kernel(core_ref, z_ref, own_ref, other_ref, *refs):
    z = z_ref[0]
    count = own_ref.shape[0]
    first_out, out_refs = refs[-1 - count], refs[-count:]

    def go(first_ref, second_ref):
        for r, out_ref in enumerate(out_refs):
            a, b = compose_into(second_ref[z ^ r], first_ref[z ^ r])
            out_ref[:, :DK] = a
            out_ref[:, DK:] = b
        first_out[...] = first_ref[...]

    @pl.when(core_ref[0] == 0)
    def _():
        go(own_ref, other_ref)

    @pl.when(core_ref[0] != 0)
    def _():
        go(other_ref, own_ref)


def chip_maps(core, z, own, other, after=()):
    return call(
        chip_kernel,
        "chip_maps",
        [core, z, own, other, *after],
        [SCALAR, SCALAR, VECTOR, VECTOR] + [ANYWHERE] * len(after),
        (shaped(*own.shape),) + (shaped(DK, DK + DV),) * own.shape[0],
    )


def group_kernel(rounds, z_ref, *refs):
    z = z_ref[0]
    in_refs = refs[:rounds]
    total_ref, prefix_ref, ordered_ref = refs[-3:]
    for r in range(rounds):
        ordered_ref[z ^ r] = in_refs[r][...]
    running = ordered_ref[0]
    for k in range(1, rounds):
        prefix_ref[k - 1] = running
        a, b = compose_into(ordered_ref[k], running)
        running = jnp.concatenate([a, b], axis=1)
    total_ref[...] = running


def group_maps(z, pieces, after=()):
    rounds = len(pieces)
    return call(
        functools.partial(group_kernel, rounds),
        "group_maps",
        [z, *pieces, *after],
        [SCALAR] + [VECTOR] * rounds + [ANYWHERE] * len(after),
        (shaped(DK, DK + DV), shaped(rounds - 1, DK, DK + DV)),
        scratch=[pltpu.VMEM((rounds, DK, DK + DV), F32)],
    )


def state_kernel(
    start, count, groups, core_ref, z_ref, group_ref, initial_ref, prefix_ref, *refs
):
    z, group = z_ref[0], group_ref[0]
    ordered_ref = refs[-1]
    out_refs = refs[-1 - count : -1]
    in_refs = refs[:groups]
    for r, ref in enumerate(in_refs):
        ordered_ref[group ^ r] = ref[...]

    def advance(k, state):
        return mul(ordered_ref[k, :, :DK], state) + ordered_ref[k, :, DK:]

    state = lax.fori_loop(0, group, advance, initial_ref[core_ref[0] * HALF + start + z])
    for r, out_ref in enumerate(out_refs):
        spot = z ^ r
        back = jnp.maximum(spot - 1, 0)
        moved = mul(prefix_ref[back, :, :DK], state) + prefix_ref[back, :, DK:]
        out_ref[...] = jnp.where(spot == 0, state, moved)


def chip_states(start, count, core, z, group, initial, prefix, groups, after=()):
    return call(
        functools.partial(state_kernel, start, count, len(groups)),
        "chip_states",
        [core, z, group, initial, prefix, *groups, *after],
        [SCALAR] * 3 + [VECTOR] * (2 + len(groups)) + [ANYWHERE] * len(after),
        (shaped(DK, DV),) * count,
        scratch=[
            pltpu.VMEM((len(groups), DK, DK + DV), F32),
        ],
    )


def core_kernel(core_ref, z_ref, first_ref, *refs):
    z = z_ref[0]
    count = first_ref.shape[0]
    in_refs = refs[:count]
    keep_ref, give_ref = refs[-2:]

    def go(start_ref, later_ref):
        for r, ref in enumerate(in_refs):
            state = ref[...]
            start_ref[z ^ r] = state
            later_ref[z ^ r] = mul(first_ref[z ^ r, :, :DK], state) + first_ref[z ^ r, :, DK:]

    @pl.when(core_ref[0] == 0)
    def _():
        go(keep_ref, give_ref)

    @pl.when(core_ref[0] != 0)
    def _():
        go(give_ref, keep_ref)


def core_states(core, z, first, pieces, after=()):
    out = shaped(len(pieces), DK, DV)
    return call(
        core_kernel,
        "core_states",
        [core, z, first, *pieces, *after],
        [SCALAR] * 2 + [VECTOR] * (1 + len(pieces)) + [ANYWHERE] * len(after),
        (out, out),
    )


def matmul(left, right):
    return jnp.einsum("...ij,...jk->...ik", left, right, precision=HIGHEST)


def gathered_states(maps, initial):
    seq, grp = lax.axis_size("seq"), lax.axis_size("grp")
    place, group = lax.axis_index("seq"), lax.axis_index("grp")

    def compose(before, step):
        both = matmul(step[..., :DK], before)
        return both.at[..., DK:].add(step[..., DK:])

    heads = maps.shape[0]
    identity = jnp.concatenate(
        [jnp.eye(DK, dtype=F32), jnp.zeros((DK, DV), F32)], axis=1
    )
    identity = jnp.broadcast_to(identity, (heads, DK, DK + DV))
    everything = lax.all_gather(maps, "seq")

    def lap(k, carry):
        total, mine = carry
        mine = jnp.where(k == place, total, mine)
        return compose(total, everything[k]), mine

    total, mine = lax.fori_loop(0, seq, lap, (identity, identity))
    groups = lax.all_gather(total, "grp")

    def step(k, state):
        return matmul(groups[k][..., :DK], state) + groups[k][..., DK:]

    start = lax.fori_loop(0, group, step, initial)
    return matmul(mine[..., :DK], start) + mine[..., DK:]


def swap_pairs(size, bit):
    return [(i, i ^ bit) for i in range(size)]


def body(
    query_proj, key_proj, value_proj, log_decay, write_rate, gate_proj, norm_gain, initial_state
):
    seq, grp = lax.axis_size("seq"), lax.axis_size("grp")
    chips = seq // 2
    place = lax.axis_index("seq")
    group = lax.axis_index("grp").astype(jnp.int32).reshape(1)
    core, z = (place % 2).astype(jnp.int32).reshape(1), (place // 2).astype(jnp.int32).reshape(1)
    gain = norm_gain.reshape(1, DV)
    mine, theirs = core, 1 - core
    decays, rates = log_decay.T, write_rate.T
    fast = seq % 2 == 0 and chips in (2, 4, 8) and grp & (grp - 1) == 0

    def maps_of(side, start, count, **options):
        return make_maps(side, start, count, key_proj, value_proj, decays, rates, **options)

    def terms_of(side, start, count, inverse, after=()):
        return make_readout(
            side, start, count, query_proj, key_proj, value_proj, decays, rates, inverse, after
        )

    out = None
    if not fast:
        maps_mine, solved_mine = maps_of(mine, 0, HALF)
        maps_theirs, solved_theirs = maps_of(theirs, 0, HALF)
        maps = jnp.where(
            core[0] == 0,
            jnp.concatenate([maps_mine, maps_theirs]),
            jnp.concatenate([maps_theirs, maps_mine]),
        )
        state = gathered_states(maps, initial_state)
        for side, solved in ((mine, solved_mine), (theirs, solved_theirs)):
            part = lax.dynamic_slice_in_dim(state, side[0] * HALF, HALF)
            terms = terms_of(side, 0, HALF, solved)
            out = finish(side, 0, HALF, *terms, part, gate_proj, gain, out)
        return out

    starts = range(0, HALF, chips)
    firsts, inverses, pieces, terms, after = [], [], [], [], ()
    for k, start in enumerate(starts):
        scalars = (mine, z, group) if k == 0 else None
        maps_theirs, inverse_theirs = maps_of(theirs, start, chips, after=after, scalars=scalars)
        other = lax.ppermute(maps_theirs, "seq", swap_pairs(seq, 1))
        maps_mine, inverse_mine = maps_of(mine, start, chips, after=(inverse_theirs,))
        inverses += [(mine, start, inverse_mine), (theirs, start, inverse_theirs)]
        first, *chip = chip_maps(core, z, maps_mine, other)
        firsts.append(first)
        after = (chip[0],)
        pieces.append(
            [chip[0]]
            + [lax.ppermute(chip[r], "seq", swap_pairs(seq, 2 * r)) for r in range(1, chips)]
        )
    prefixes, groups = [], []
    for k, start in enumerate(starts):
        total, prefix = group_maps(z, pieces[k], after)
        prefixes.append(prefix)
        groups.append(
            [total] + [lax.ppermute(total, "grp", swap_pairs(grp, r)) for r in range(1, grp)]
        )
        after = (total,)
        if k == 0:
            for side, begin, inverse in inverses:
                terms.append(terms_of(side, begin, chips, inverse, after))
                after = (terms[-1][0],)
    backs = []
    for k, start in enumerate(starts):
        back = chip_states(
            start, chips, core, z, group, initial_state, prefixes[k], groups[k], after
        )
        after = (back[0],)
        backs.append(
            [back[0]]
            + [lax.ppermute(back[r], "seq", swap_pairs(seq, 2 * r)) for r in range(1, chips)]
        )
    for k, start in enumerate(starts):
        state, give = core_states(core, z, firsts[k], backs[k], after)
        states = (state, lax.ppermute(give, "seq", swap_pairs(seq, 1)))
        for part, side in enumerate((mine, theirs)):
            out = finish(
                side, start, chips, *terms[2 * k + part], states[part], gate_proj, gain, out
            )
        after = (pltpu.with_memory_space_constraint(out, pltpu.HBM),)
    return out


def solution(mesh):
    spread = P(("grp", "seq"), None)
    placed = (spread,) * 6 + (P(), P())
    return jax.shard_map(body, mesh=mesh, in_specs=placed, out_specs=spread, check_vma=False)
```
